32 devices in a mesh: row: 4 (over y, x), col: 8 (over z, core).
Axes of the slice: x: 2, y: 2, z: 4, core: 2. Of those that a mesh axis runs over, the one named last changes fastest.
Arguments:
- xblocks: bfloat16 [56, 8, 128, 128], P('row', 'col'), may hold values from -2 to 2
- xcols: int32 [56, 8], P('row', 'col'), may hold values from 0 to 6, as said below
- outcols: int32 [56, 16], P('row', 'col'), may hold values from 0 to 6, as said below
Outputs:
- square_blocks: bfloat16 [56, 16, 128, 128], P('row', 'col')
The draws below stay inside these ranges and needn't reach their ends.
Inputs may be any that keep to these rules, and one draw needn't show every extreme that they name: xcols[m, t] is a block column within column tile t; over all block rows, the entries of one column tile take at most 3 distinct values. `outcols`: each entry names a block column of its column tile at which at least one block product of the window for that block row lands; entries of one row and tile may repeat.
All inputs are finite; a program needn't handle non-finite values.
Results may differ from the reference program's by a relative error of at most 0.001.
Values may be sent and summed in bfloat16 or wider, within the bound.
A program may use at most 64 MiB of HBM per device.

```python
import jax
import jax.numpy as jnp
from jax import lax

BS = 128
BLK_C = 7
KO = 2
LAND = 3
STEPS = 4
BLK_R = 14
NBLK = 56
N_ROW = 4
N_COL = 8


def draw_pattern(key):
    stride = BLK_C // LAND
    top_base = BLK_C - 1 - (LAND - 1) * stride
    base = jax.random.randint(jax.random.fold_in(key, 7), (N_COL,), 0, BLK_C, dtype=jnp.int32)
    base = base.at[0].set(top_base).at[1].set(0)
    steps_drawn = jax.random.randint(jax.random.fold_in(key, 11), (NBLK, N_COL), 0, LAND, dtype=jnp.int32)
    return ((base[None, :] + steps_drawn * stride) % BLK_C).astype(jnp.int32)


def draw_xcols(key, part):
    return draw_pattern(key)


def draw_outcols(key, part):
    pattern = draw_pattern(key)
    per_panel = N_COL // N_ROW
    count = STEPS * per_panel
    slots = jnp.arange(count, dtype=jnp.int32)
    step_ids = slots // per_panel
    half_ids = slots % per_panel
    grid_row = jnp.arange(NBLK, dtype=jnp.int32) // BLK_R
    panel = (grid_row[:, None] + step_ids[None, :]) % N_ROW
    tiles = per_panel * panel + half_ids[None, :]
    a_cols = jnp.take_along_axis(pattern, tiles, axis=1)
    b_rows = panel * BLK_R + half_ids[None, :] * BLK_C + a_cols
    landing = jnp.transpose(pattern[b_rows], (0, 2, 1))
    picks = jax.random.randint(jax.random.fold_in(key, 23), (NBLK, N_COL, KO), 0, count, dtype=jnp.int32)
    chosen = jnp.take_along_axis(landing, picks, axis=2)
    return chosen.reshape(NBLK, N_COL * KO).astype(jnp.int32)


def steps_of(own_key, shape, cuts, low, largest):
    def one(axis_at, shards_of):
        steps = jax.random.uniform(jax.random.fold_in(jax.random.fold_in(own_key, 6), axis_at), (shards_of,), jnp.float32, low / len(cuts), largest / len(cuts))
        return jnp.repeat(jnp.exp(steps), shape[axis_at] // shards_of).reshape((-1,) + (1,) * (len(shape) - axis_at - 1))

    level = one(*cuts[0])
    for cut in cuts[1:]:
        level = level * one(*cut)
    return level


def centred(stream_key, extent, scale, bound, pieces=(), kind=jnp.bfloat16):
    level = steps_of(stream_key, extent, pieces, -0.22, 0.18) if pieces else 1.0
    values = jax.random.normal(stream_key, extent, jnp.float32) * scale * level
    return jnp.minimum(jnp.maximum(values, -bound), bound).astype(kind)


def setup_inputs(seed: int = 0) -> dict:
    seeds = jax.random.split(jax.random.key(seed), 4)
    return {
        "xblocks": centred(seeds[0], (NBLK, N_COL, BS, BS), 0.3, 2.0, ((0, 4), (1, 8))),
        "xcols": draw_xcols(jax.random.fold_in(seeds[3], 71), 0),
        "outcols": draw_outcols(jax.random.fold_in(seeds[3], 71), 0),
    }


def reference(xblocks, xcols, outcols):
    per_panel = N_COL // N_ROW
    step_ids = jnp.arange(STEPS, dtype=jnp.int32)
    half_ids = jnp.arange(per_panel, dtype=jnp.int32)

    def one_row(block_row):
        grid_row = block_row // BLK_R
        panel = (grid_row + step_ids[:, None]) % N_ROW
        tiles = (per_panel * panel + half_ids[None, :]).reshape(-1).astype(jnp.int32)
        a_blocks = xblocks[block_row][tiles].astype(jnp.float32)
        a_cols = xcols[block_row][tiles]
        b_rows = ((panel * BLK_R + half_ids[None, :] * BLK_C).reshape(-1) + a_cols).astype(jnp.int32)
        b_blocks = xblocks[b_rows].astype(jnp.float32)
        landing = xcols[b_rows]
        targets = outcols[block_row].reshape(N_COL, KO)
        weight = (landing[:, :, None] == targets[None, :, :]).astype(jnp.float32)
        products = jnp.einsum('qab,qjbc->qjac', a_blocks, b_blocks, precision=lax.Precision.HIGHEST)
        summed = jnp.einsum('qjo,qjac->joac', weight, products, precision=lax.Precision.HIGHEST)
        return summed.reshape(N_COL * KO, BS, BS).astype(jnp.bfloat16)

    return lax.map(one_row, jnp.arange(NBLK, dtype=jnp.int32))
```

```python
import functools

import jax
import jax.numpy as jnp
from jax import lax
from jax.experimental import pallas as pl
from jax.experimental.pallas import tpu as pltpu
from jax.sharding import PartitionSpec as P

STEPS = 4
CORES = 2
MESH = pl.DeviceIdType.MESH


def passed_along(value, axis, steps):
    count = lax.axis_size(axis)
    pairs = [(source, (source + steps) % count) for source in range(count)]
    return lax.ppermute(value, axis, pairs)


def broadcast(value, axis, source):
    kept = jnp.where(lax.axis_index(axis) == source, value, 0).astype(value.dtype)
    return lax.psum(kept, axis)


def add_products(total, a_blocks, a_cols, b_blocks, b_cols, targets, offset):
    index = offset + a_cols
    chosen = jnp.take(b_blocks, index, axis=0)
    landing = jnp.take(b_cols, index, axis=0)
    product = jnp.einsum("mab,mbc->mac", a_blocks, chosen, preferred_element_type=jnp.float32)
    weight = (landing[:, None] == targets).astype(jnp.float32)
    return total + weight[:, :, None, None] * product[:, None]


def on_any_mesh(xblocks, xcols, outcols):
    row_count = lax.axis_size("row")
    col_count = lax.axis_size("col")
    per_panel = col_count // row_count
    block_rows = xblocks.shape[0]
    tile_cols = block_rows // per_panel
    block_size = xblocks.shape[2]
    kept = outcols.shape[1]
    row_here = lax.axis_index("row")
    own_blocks = xblocks[:, 0]
    own_cols = xcols[:, 0]
    total = jnp.zeros((block_rows, kept, block_size, block_size), jnp.float32)
    moving = (own_blocks, own_cols)
    for step_no in range(STEPS):
        panel = (row_here + step_no) % row_count
        if step_no > 0:
            moving = passed_along((moving[0], moving[1]), "row", -1)
        for half_no in range(per_panel):
            tile_blocks, tile_cols_ids = (
                broadcast(own_blocks, "col", per_panel * panel + half_no),
                broadcast(own_cols, "col", per_panel * panel + half_no),
            )
            total = add_products(
                total,
                tile_blocks,
                tile_cols_ids,
                moving[0],
                moving[1],
                outcols,
                half_no * tile_cols,
            )
    return total.astype(jnp.bfloat16)


def remote(src, dst, send_sem, recv_sem, row, col):
    return pltpu.make_async_remote_copy(
        src_ref=src,
        dst_ref=dst,
        send_sem=send_sem,
        recv_sem=recv_sem,
        device_id=(row, col),
        device_id_type=MESH,
    )


def kernel(
    xc_ref, oc_ref, x_ref, o_ref,
    a_buf, b_buf, acc, meta_v, meta_s,
    meta_send, meta_recv, meta_loc, own_loc,
    right_send, left_send, lane_recv, sib_send, sib_recv,
    row_send, row_fwd, row_recv,
):
    rows = x_ref.shape[0]
    half = rows // 2
    chips = STEPS
    i = lax.axis_index("row")
    j = lax.axis_index("col")
    z, c = j // CORES, j % CORES
    y, x = i // 2, i % 2
    xn = 2 * y + (1 - x)
    yn = 2 * (1 - y) + x
    dg = 2 * (1 - y) + (1 - x)
    row_peers = (xn, yn, dg)
    col_peers = [lax.rem(j + d, CORES * chips) for d in range(1, CORES * chips)]

    barrier = pltpu.get_barrier_semaphore()
    for r in row_peers:
        pl.semaphore_signal(barrier, inc=1, device_id=(r, j), device_id_type=MESH)
    for q in col_peers:
        pl.semaphore_signal(barrier, inc=1, device_id=(i, q), device_id_type=MESH)

    lane = lax.broadcasted_iota(jnp.int32, (8, 128), 1)
    vec = jnp.zeros((8, 128), jnp.int32)
    for m in range(rows):
        vec = jnp.where(lane == m, xc_ref[m, 0], vec)
    meta_v[j] = vec
    meta_v[CORES * chips + i] = vec
    own = pltpu.make_async_copy(x_ref.at[:, 0], a_buf.at[j], own_loc.at[0])
    own_b = pltpu.make_async_copy(x_ref.at[:, 0], b_buf.at[i], own_loc.at[1])
    own.start()
    own_b.start()
    pl.semaphore_wait(barrier, len(row_peers) + len(col_peers))

    metas = []
    slot = CORES * chips + i
    for n, r in enumerate(row_peers):
        metas.append(
            (remote(meta_v.at[slot], meta_v.at[slot], meta_send.at[n], meta_recv.at[slot], r, j), CORES * chips + r)
        )
    for n, q in enumerate(col_peers):
        metas.append((remote(meta_v.at[j], meta_v.at[j], meta_send.at[3 + n], meta_recv.at[j], i, q), q))
    for copy, _ in metas:
        copy.start()

    def part(k):
        return pl.ds(k * half, half)

    def own_part(k):
        return x_ref.at[part(k), 0]

    def a_part(zs, core, k):
        return a_buf.at[CORES * zs + core, part(k)]

    def src_of(d, zs, k):
        return own_part(k) if d == 0 else a_part(zs, c, k)

    def to_right(d, zs, k):
        return remote(
            src_of(d, zs, k), a_part(zs, c, k), right_send.at[d, k], lane_recv.at[zs, k], i, j + CORES
        )

    def to_left(d, zs, k):
        return remote(
            src_of(d, zs, k), a_part(zs, c, k), left_send.at[d, k], lane_recv.at[zs, k], i, j - CORES
        )

    def to_sib(d, zs, k):
        return remote(
            src_of(d, zs, k), a_part(zs, c, k), sib_send.at[zs, k], sib_recv.at[zs, k], i, j + 1 - 2 * c
        )

    def lane_wait(zs, k):
        remote(a_part(zs, c, k), a_part(zs, c, k), sib_send.at[zs, k], lane_recv.at[zs, k], i, j + 1 - 2 * c).wait_recv()

    def sib_wait(zs, k):
        there = a_part(zs, 1 - c, k)
        remote(there, there, sib_send.at[zs, k], sib_recv.at[zs, k], i, j + 1 - 2 * c).wait_recv()

    def b_part(p, k):
        return b_buf.at[p, part(k)]

    def row_copy(n, k):
        return remote(own_part(k), b_part(i, k), row_send.at[n, k], row_recv.at[i, k], row_peers[n], j)

    def row_wait(p, k):
        remote(b_part(p, k), b_part(p, k), row_fwd.at[0], row_recv.at[p, k], xn, j).wait_recv()

    fwd_y = remote(b_part(xn, 0), b_part(xn, 0), row_fwd.at[0], row_recv.at[xn, 0], yn, j)
    fwd_x = remote(b_part(yn, 1), b_part(yn, 1), row_fwd.at[1], row_recv.at[yn, 1], xn, j)

    inner_right = z < chips - 1
    inner_left = z > 0
    for k in range(2):
        pl.when(inner_right)(lambda k=k: to_right(0, z, k).start())
        pl.when(inner_left)(lambda k=k: to_left(0, z, k).start())
        row_copy(0, k).start()
        row_copy(1, 1 - k).start()
    for k in range(2):
        to_sib(0, z, k).start()

    for d in (1, 2, 3):
        for k in range(2):
            def from_left(d=d, k=k):
                lane_wait(z - d, k)
                pl.when(inner_right)(lambda: to_right(d, z - d, k).start())
                to_sib(d, z - d, k).start()

            def from_right(d=d, k=k):
                lane_wait(z + d, k)
                pl.when(inner_left)(lambda: to_left(d, z + d, k).start())
                to_sib(d, z + d, k).start()

            if d < 3:
                pl.when(z - d >= 0)(from_left)
                pl.when(z + d <= chips - 1)(from_right)
            if d == 1 and k == 0:
                row_wait(xn, 0)
                fwd_y.start()
                row_wait(yn, 1)
                fwd_x.start()
                for copy, source in metas:
                    there = meta_v.at[source]
                    remote(there, there, meta_send.at[0], meta_recv.at[source], xn, j).wait_recv()
                for copy, _ in metas:
                    copy.wait_send()
                down = pltpu.make_async_copy(meta_v, meta_s, meta_loc)
                down.start()
                down.wait()

    row_wait(xn, 1)
    row_wait(yn, 0)
    row_wait(dg, 0)
    row_wait(dg, 1)
    own.wait()
    own_b.wait()

    first = z // 2
    last = (chips - 1) * (1 - first)

    def operands(m, zs):
        left, right = [], []
        for h in range(CORES):
            t = CORES * zs + h
            at = h * half + meta_s[t, 0, m]
            block = b_buf[zs, at]
            landing = meta_s[CORES * chips + zs, 0, at]
            zero = jnp.zeros_like(block)
            right.append(
                jnp.concatenate(
                    [jnp.where(landing == oc_ref[m, o], block, zero) for o in range(2)], axis=1
                )
            )
            left.append(a_buf[t, m])
        return left, right

    def product(m, sources):
        left, right = [], []
        for zs in sources:
            more = operands(m, zs)
            left += more[0]
            right += more[1]
        return jnp.dot(
            jnp.concatenate(left, axis=1), jnp.concatenate(right, axis=0), preferred_element_type=jnp.float32
        )

    def near(n):
        return n + first

    def wait_sib_near(k):
        for n in range(chips - 1):
            sib_wait(near(n), k)

    far = last

    def far_lane(k):
        def from_left():
            lane_wait(0, k)
            to_sib(3, far, k).start()

        def from_right():
            lane_wait(chips - 1, k)
            to_sib(3, far, k).start()

        pl.when(z == chips - 1)(from_left)
        pl.when(z == 0)(from_right)

    def early(m, carry):
        acc[m] = product(m, [near(n) for n in range(chips - 1)])
        return carry

    def late(m, carry):
        total = acc[m] + product(m, [far])
        for o in range(2):
            o_ref[m, o] = total[:, o * 128 : (o + 1) * 128].astype(o_ref.dtype)
        return carry

    for k in range(2):
        wait_sib_near(k)
        lax.fori_loop(k * half, (k + 1) * half, early, 0)
    for k in range(2):
        far_lane(k)
        sib_wait(far, k)
        lax.fori_loop(k * half, (k + 1) * half, late, 0)

    for k in range(2):
        for n in range(2):
            row_copy(n, k).wait_send()
        for d in range(chips):
            def right_done(d=d, k=k):
                to_right(d, z - d, k).wait_send()

            def left_done(d=d, k=k):
                to_left(d, z + d, k).wait_send()

            if d < chips - 1:
                pl.when(jnp.logical_and(inner_right, z - d >= 0))(right_done)
                pl.when(jnp.logical_and(inner_left, z + d <= chips - 1))(left_done)
            to_sib(1, d, k).wait_send()
    fwd_y.wait_send()
    fwd_x.wait_send()


def on_four_by_eight(xblocks, xcols, outcols):
    rows, _, size, _ = xblocks.shape
    kept = outcols.shape[1]
    slots = CORES * STEPS + STEPS
    dma = pltpu.SemaphoreType.DMA
    return pl.pallas_call(
        kernel,
        out_shape=jax.ShapeDtypeStruct((rows, kept, size, size), jnp.bfloat16),
        in_specs=[
            pl.BlockSpec(memory_space=pltpu.SMEM),
            pl.BlockSpec(memory_space=pltpu.SMEM),
            pl.BlockSpec(memory_space=pltpu.VMEM),
        ],
        out_specs=pl.BlockSpec(memory_space=pltpu.VMEM),
        scratch_shapes=[
            pltpu.VMEM((CORES * STEPS, rows, size, size), jnp.bfloat16),
            pltpu.VMEM((STEPS, rows, size, size), jnp.bfloat16),
            pltpu.VMEM((rows, size, kept * size), jnp.float32),
            pltpu.VMEM((slots, 8, 128), jnp.int32),
            pltpu.SMEM((slots, 8, 128), jnp.int32),
            dma((10,)),
            dma((slots,)),
            dma,
            dma((2,)),
            dma((STEPS, 2)),
            dma((STEPS, 2)),
            dma((STEPS, 2)),
            dma((STEPS, 2)),
            dma((STEPS, 2)),
            dma((2, 2)),
            dma((2,)),
            dma((STEPS, 2)),
        ],
        compiler_params=pltpu.CompilerParams(
            collective_id=0, has_side_effects=True, vmem_limit_bytes=32 * 1024 * 1024
        ),
    )(xcols, outcols, xblocks)


def solution(mesh):
    in_specs = (P("row", "col", None, None), P("row", "col"), P("row", "col"))
    out_specs = P("row", "col", None, None)
    fits = mesh.shape["row"] == STEPS and mesh.shape["col"] == CORES * STEPS
    body = on_four_by_eight if fits else on_any_mesh
    return jax.shard_map(body, mesh=mesh, in_specs=in_specs, out_specs=out_specs, check_vma=False)
```

```python
import functools

import jax
import jax.numpy as jnp
from jax import lax
from jax.experimental import pallas as pl
from jax.experimental.pallas import tpu as pltpu
from jax.sharding import PartitionSpec as P

STEPS = 4
CORES = 2
PIECE = 2
MESH = pl.DeviceIdType.MESH


def passed_along(value, axis, steps):
    count = lax.axis_size(axis)
    pairs = [(source, (source + steps) % count) for source in range(count)]
    return lax.ppermute(value, axis, pairs)


def broadcast(value, axis, source):
    kept = jnp.where(lax.axis_index(axis) == source, value, 0).astype(value.dtype)
    return lax.psum(kept, axis)


def add_products(total, a_blocks, a_cols, b_blocks, b_cols, targets, offset):
    index = offset + a_cols
    chosen = jnp.take(b_blocks, index, axis=0)
    landing = jnp.take(b_cols, index, axis=0)
    product = jnp.einsum("mab,mbc->mac", a_blocks, chosen, preferred_element_type=jnp.float32)
    weight = (landing[:, None] == targets).astype(jnp.float32)
    return total + weight[:, :, None, None] * product[:, None]


def on_any_mesh(xblocks, xcols, outcols):
    row_count = lax.axis_size("row")
    col_count = lax.axis_size("col")
    per_panel = col_count // row_count
    block_rows = xblocks.shape[0]
    tile_cols = block_rows // per_panel
    block_size = xblocks.shape[2]
    kept = outcols.shape[1]
    row_here = lax.axis_index("row")
    own_blocks = xblocks[:, 0]
    own_cols = xcols[:, 0]
    total = jnp.zeros((block_rows, kept, block_size, block_size), jnp.float32)
    moving = (own_blocks, own_cols)
    for step_no in range(STEPS):
        panel = (row_here + step_no) % row_count
        if step_no > 0:
            moving = passed_along((moving[0], moving[1]), "row", -1)
        for half_no in range(per_panel):
            tile_blocks, tile_cols_ids = (
                broadcast(own_blocks, "col", per_panel * panel + half_no),
                broadcast(own_cols, "col", per_panel * panel + half_no),
            )
            total = add_products(
                total,
                tile_blocks,
                tile_cols_ids,
                moving[0],
                moving[1],
                outcols,
                half_no * tile_cols,
            )
    return total.astype(jnp.bfloat16)


def remote(src, dst, send_sem, recv_sem, row, col):
    return pltpu.make_async_remote_copy(
        src_ref=src,
        dst_ref=dst,
        send_sem=send_sem,
        recv_sem=recv_sem,
        device_id=(row, col),
        device_id_type=MESH,
    )


def kernel(
    xc_ref, oc_ref, x_ref, o_ref,
    a_buf, b_buf, acc, meta_v, meta_s, oc_s,
    meta_loc, own_loc,
    right_send, left_send, lane_recv, sib_send, sib_recv,
    row_send, row_fwd, row_recv,
):
    rows = x_ref.shape[0]
    half = rows // 2
    chips = STEPS
    pieces = rows // PIECE
    meta = pieces
    i = lax.axis_index("row")
    j = lax.axis_index("col")
    z, c = j // CORES, j % CORES
    y, x = i // 2, i % 2
    xn = 2 * y + (1 - x)
    yn = 2 * (1 - y) + x
    dg = 2 * (1 - y) + (1 - x)
    sib = j + 1 - 2 * c
    right, left = j + CORES, j - CORES
    inner_right = z < chips - 1
    inner_left = z > 0
    tiles = CORES * chips

    barrier = pltpu.get_barrier_semaphore()

    def greet(row, col):
        pl.semaphore_signal(barrier, inc=1, device_id=(row, col), device_id_type=MESH)

    greet(i, sib)
    pl.when(inner_right)(lambda: greet(i, right))
    pl.when(inner_left)(lambda: greet(i, left))
    greet(xn, j)
    greet(yn, j)

    own = pltpu.make_async_copy(x_ref.at[:, 0], a_buf.at[j], own_loc.at[0])
    own_b = pltpu.make_async_copy(x_ref.at[:, 0], b_buf.at[i], own_loc.at[1])
    own.start()
    own_b.start()
    oc_down = pltpu.make_async_copy(oc_ref, oc_s, own_loc.at[2])
    oc_down.start()
    meta_v[j, 0:1, 0:rows] = xc_ref[...]
    meta_v[tiles + i, 0:1, 0:rows] = xc_ref[...]
    pl.semaphore_wait(barrier, 5 - jnp.where(jnp.logical_and(inner_left, inner_right), 0, 1))

    def part(k):
        return pl.ds(k * PIECE, PIECE)

    def there(zs, core, k):
        if k is meta:
            return meta_v.at[CORES * zs + core]
        return a_buf.at[CORES * zs + core, part(k)]

    def here(d, zs, k):
        if k is meta or d != 0:
            return there(zs, c, k)
        return x_ref.at[part(k), 0]

    def to_right(d, zs, k):
        return remote(here(d, zs, k), there(zs, c, k), right_send.at[d, k], lane_recv.at[zs, k], i, right)

    def to_left(d, zs, k):
        return remote(here(d, zs, k), there(zs, c, k), left_send.at[d, k], lane_recv.at[zs, k], i, left)

    def to_sib(d, zs, k):
        return remote(here(d, zs, k), there(zs, c, k), sib_send.at[zs, k], sib_recv.at[zs, k], i, sib)

    def lane_wait(zs, k):
        remote(there(zs, c, k), there(zs, c, k), sib_send.at[zs, k], lane_recv.at[zs, k], i, sib).wait_recv()

    def sib_wait(zs, k):
        mine = there(zs, 1 - c, k)
        remote(mine, mine, sib_send.at[zs, k], sib_recv.at[zs, k], i, sib).wait_recv()

    def b_part(p, k):
        if k == 2:
            return meta_v.at[tiles + p]
        return b_buf.at[p, pl.ds(k * half, half)]

    def row_copy(n, k):
        source = b_part(i, k) if k == 2 else x_ref.at[pl.ds(k * half, half), 0]
        return remote(source, b_part(i, k), row_send.at[n, k], row_recv.at[i, k], (xn, yn)[n], j)

    def row_wait(p, k):
        remote(b_part(p, k), b_part(p, k), row_fwd.at[0], row_recv.at[p, k], xn, j).wait_recv()

    def row_forward(n, k):
        p, to = ((xn, yn), (yn, xn))[n]
        return remote(b_part(p, k), b_part(p, k), row_fwd.at[k], row_recv.at[p, k], to, j)

    forwards = [row_forward(0, 0), row_forward(1, 1), row_forward(0, 2)]

    def own_out(k):
        pl.when(inner_right)(lambda: to_right(0, z, k).start())
        pl.when(inner_left)(lambda: to_left(0, z, k).start())

    own_out(meta)
    row_copy(0, 2).start()
    row_copy(1, 2).start()
    lax.fori_loop(0, pieces, lambda k, n: (own_out(k), n)[1], 0)
    for k in range(2):
        row_copy(0, k).start()
        row_copy(1, 1 - k).start()
    to_sib(0, z, meta).start()
    lax.fori_loop(0, pieces, lambda k, n: (to_sib(0, z, k).start(), n)[1], 0)

    def from_left(d, k):
        lane_wait(z - d, k)
        if d < chips - 1:
            pl.when(inner_right)(lambda: to_right(d, z - d, k).start())
        to_sib(d, z - d, k).start()

    def from_right(d, k):
        lane_wait(z + d, k)
        if d < chips - 1:
            pl.when(inner_left)(lambda: to_left(d, z + d, k).start())
        to_sib(d, z + d, k).start()

    def arrive(d, k):
        pl.when(z - d >= 0)(lambda: from_left(d, k))
        pl.when(z + d <= chips - 1)(lambda: from_right(d, k))

    def arrive_loop(d):
        arrive(d, meta)
        lax.fori_loop(0, pieces, lambda k, n: (arrive(d, k), n)[1], 0)

    arrive_loop(1)
    row_wait(xn, 2)
    forwards[2].start()
    row_wait(xn, 0)
    forwards[0].start()
    row_wait(yn, 1)
    forwards[1].start()
    arrive_loop(2)
    row_wait(yn, 2)
    row_wait(dg, 2)
    row_wait(xn, 1)
    row_wait(yn, 0)
    row_wait(dg, 0)
    row_wait(dg, 1)
    own.wait()
    own_b.wait()
    oc_down.wait()

    first = z // 2
    far = (chips - 1) * (1 - first)

    def near(n):
        return n + first

    def lower(start, count):
        down = pltpu.make_async_copy(meta_v.at[pl.ds(start, count)], meta_s.at[pl.ds(start, count)], meta_loc)
        down.start()
        down.wait()

    for n in range(chips - 1):
        sib_wait(near(n), meta)
    lower(CORES * first, CORES * (chips - 1))
    lower(tiles, chips)

    def operands(m, zs):
        lhs, rhs = [], []
        for h in range(CORES):
            t = CORES * zs + h
            at = h * half + meta_s[t, 0, m]
            block = b_buf[zs, at]
            landing = meta_s[tiles + zs, 0, at]
            zero = jnp.zeros_like(block)
            rhs.append(
                jnp.concatenate([jnp.where(landing == oc_s[o, m], block, zero) for o in range(2)], axis=1)
            )
            lhs.append(a_buf[t, m])
        return lhs, rhs

    def product(m, sources):
        lhs, rhs = [], []
        for zs in sources:
            more = operands(m, zs)
            lhs += more[0]
            rhs += more[1]
        return jnp.dot(
            jnp.concatenate(lhs, axis=1), jnp.concatenate(rhs, axis=0), preferred_element_type=jnp.float32
        )

    def early(k, carry):
        for n in range(chips - 1):
            sib_wait(near(n), k)
        for r in range(PIECE):
            m = k * PIECE + r
            acc[m] = product(m, [near(n) for n in range(chips - 1)])
        return carry

    lax.fori_loop(0, pieces, early, 0)

    def far_arrive(k):
        pl.when(z == chips - 1)(lambda: from_left(chips - 1, k))
        pl.when(z == 0)(lambda: from_right(chips - 1, k))

    far_arrive(meta)
    far_arrive(0)
    sib_wait(far, meta)
    lower(CORES * far, CORES)

    def late(k, carry):
        pl.when(k < pieces - 1)(lambda: far_arrive(jnp.minimum(k + 1, pieces - 1)))
        sib_wait(far, k)
        for r in range(PIECE):
            m = k * PIECE + r
            total = acc[m] + product(m, [far])
            for o in range(2):
                o_ref[m, o] = total[:, o * 128 : (o + 1) * 128].astype(o_ref.dtype)
        return carry

    lax.fori_loop(0, pieces, late, 0)

    def sent(k):
        for d in range(chips):
            if d < chips - 1:
                pl.when(jnp.logical_and(inner_right, z - d >= 0))(
                    lambda d=d: to_right(d, z - d, k).wait_send()
                )
                pl.when(jnp.logical_and(inner_left, z + d <= chips - 1))(
                    lambda d=d: to_left(d, z + d, k).wait_send()
                )
            to_sib(1, d, k).wait_send()

    sent(meta)
    lax.fori_loop(0, pieces, lambda k, n: (sent(k), n)[1], 0)
    for k in range(3):
        for n in range(2):
            row_copy(n, k).wait_send()
        forwards[k].wait_send()


def on_four_by_eight(xblocks, xcols, outcols):
    rows, _, size, _ = xblocks.shape
    kept = outcols.shape[1]
    slots = CORES * STEPS + STEPS
    pieces = rows // PIECE
    dma = pltpu.SemaphoreType.DMA
    return pl.pallas_call(
        kernel,
        out_shape=jax.ShapeDtypeStruct((rows, kept, size, size), jnp.bfloat16),
        in_specs=[
            pl.BlockSpec(memory_space=pltpu.VMEM),
            pl.BlockSpec(memory_space=pltpu.VMEM),
            pl.BlockSpec(memory_space=pltpu.HBM),
        ],
        out_specs=pl.BlockSpec(memory_space=pltpu.VMEM),
        scratch_shapes=[
            pltpu.VMEM((CORES * STEPS, rows, size, size), jnp.bfloat16),
            pltpu.VMEM((STEPS, rows, size, size), jnp.bfloat16),
            pltpu.VMEM((rows, size, kept * size), jnp.float32),
            pltpu.VMEM((slots, 8, 128), jnp.int32),
            pltpu.SMEM((slots, 8, 128), jnp.int32),
            pltpu.SMEM((kept, rows), jnp.int32),
            dma,
            dma((3,)),
            dma((STEPS, pieces + 1)),
            dma((STEPS, pieces + 1)),
            dma((STEPS, pieces + 1)),
            dma((STEPS, pieces + 1)),
            dma((STEPS, pieces + 1)),
            dma((2, 3)),
            dma((3,)),
            dma((STEPS, 3)),
        ],
        compiler_params=pltpu.CompilerParams(
            collective_id=0, has_side_effects=True, vmem_limit_bytes=32 * 1024 * 1024
        ),
    )(xcols.T, outcols.T, xblocks)


def solution(mesh):
    in_specs = (P("row", "col", None, None), P("row", "col"), P("row", "col"))
    out_specs = P("row", "col", None, None)
    fits = mesh.shape["row"] == STEPS and mesh.shape["col"] == CORES * STEPS
    body = on_four_by_eight if fits else on_any_mesh
    return jax.shard_map(body, mesh=mesh, in_specs=in_specs, out_specs=out_specs, check_vma=False)
```

```python
import functools

import jax
import jax.numpy as jnp
from jax import lax
from jax.experimental import pallas as pl
from jax.experimental.pallas import tpu as pltpu
from jax.sharding import PartitionSpec as P

STEPS = 4
CORES = 2
PIECE = 2
MESH = pl.DeviceIdType.MESH


def passed_along(value, axis, steps):
    count = lax.axis_size(axis)
    pairs = [(source, (source + steps) % count) for source in range(count)]
    return lax.ppermute(value, axis, pairs)


def broadcast(value, axis, source):
    kept = jnp.where(lax.axis_index(axis) == source, value, 0).astype(value.dtype)
    return lax.psum(kept, axis)


def add_products(total, a_blocks, a_cols, b_blocks, b_cols, targets, offset):
    index = offset + a_cols
    chosen = jnp.take(b_blocks, index, axis=0)
    landing = jnp.take(b_cols, index, axis=0)
    product = jnp.einsum("mab,mbc->mac", a_blocks, chosen, preferred_element_type=jnp.float32)
    weight = (landing[:, None] == targets).astype(jnp.float32)
    return total + weight[:, :, None, None] * product[:, None]


def on_any_mesh(xblocks, xcols, outcols):
    row_count = lax.axis_size("row")
    col_count = lax.axis_size("col")
    per_panel = col_count // row_count
    block_rows = xblocks.shape[0]
    tile_cols = block_rows // per_panel
    block_size = xblocks.shape[2]
    kept = outcols.shape[1]
    row_here = lax.axis_index("row")
    own_blocks = xblocks[:, 0]
    own_cols = xcols[:, 0]
    total = jnp.zeros((block_rows, kept, block_size, block_size), jnp.float32)
    moving = (own_blocks, own_cols)
    for step_no in range(STEPS):
        panel = (row_here + step_no) % row_count
        if step_no > 0:
            moving = passed_along((moving[0], moving[1]), "row", -1)
        for half_no in range(per_panel):
            tile_blocks, tile_cols_ids = (
                broadcast(own_blocks, "col", per_panel * panel + half_no),
                broadcast(own_cols, "col", per_panel * panel + half_no),
            )
            total = add_products(
                total,
                tile_blocks,
                tile_cols_ids,
                moving[0],
                moving[1],
                outcols,
                half_no * tile_cols,
            )
    return total.astype(jnp.bfloat16)


def remote(src, dst, send_sem, recv_sem, row, col):
    return pltpu.make_async_remote_copy(
        src_ref=src,
        dst_ref=dst,
        send_sem=send_sem,
        recv_sem=recv_sem,
        device_id=(row, col),
        device_id_type=MESH,
    )


def kernel(
    xc_ref, oc_ref, x_ref, o_ref,
    a_buf, b_buf, acc, meta_v, meta_s, oc_s,
    meta_loc, own_loc,
    right_send, left_send, lane_recv, sib_send, sib_recv, meta_send,
    row_send, row_fwd, row_recv,
):
    rows = x_ref.shape[0]
    half = rows // 2
    chips = STEPS
    pieces = rows // PIECE
    meta = pieces
    i = lax.axis_index("row")
    j = lax.axis_index("col")
    z, c = j // CORES, j % CORES
    y, x = i // 2, i % 2
    xn = 2 * y + (1 - x)
    yn = 2 * (1 - y) + x
    dg = 2 * (1 - y) + (1 - x)
    sib = j + 1 - 2 * c
    right, left = j + CORES, j - CORES
    inner_right = z < chips - 1
    inner_left = z > 0
    tiles = CORES * chips

    barrier = pltpu.get_barrier_semaphore()

    def greet(row, col):
        pl.semaphore_signal(barrier, inc=1, device_id=(row, col), device_id_type=MESH)

    greet(i, sib)
    pl.when(inner_right)(lambda: greet(i, right))
    pl.when(inner_left)(lambda: greet(i, left))
    greet(xn, j)
    greet(yn, j)

    own = pltpu.make_async_copy(x_ref.at[:, 0], a_buf.at[j], own_loc.at[0])
    own_b = pltpu.make_async_copy(x_ref.at[:, 0], b_buf.at[i], own_loc.at[1])
    own.start()
    own_b.start()
    oc_down = pltpu.make_async_copy(oc_ref, oc_s, own_loc.at[2])
    oc_down.start()
    meta_v[j, 0:1, 0:rows] = xc_ref[...]
    meta_v[tiles + i, 0:1, 0:rows] = xc_ref[...]
    pl.semaphore_wait(barrier, 5 - jnp.where(jnp.logical_and(inner_left, inner_right), 0, 1))

    def part(k):
        return pl.ds(k * PIECE, PIECE)

    def there(zs, core, k):
        if k is meta:
            return meta_v.at[CORES * zs + core]
        return a_buf.at[CORES * zs + core, part(k)]

    def here(d, zs, k):
        if k is meta or d != 0:
            return there(zs, c, k)
        return x_ref.at[part(k), 0]

    def to_right(d, zs, k):
        done = meta_send.at[0, d] if k is meta else right_send.at[d]
        return remote(here(d, zs, k), there(zs, c, k), done, lane_recv.at[zs, k], i, right)

    def to_left(d, zs, k):
        done = meta_send.at[1, d] if k is meta else left_send.at[d]
        return remote(here(d, zs, k), there(zs, c, k), done, lane_recv.at[zs, k], i, left)

    def sib_slot(d, k):
        return k if k is meta or d == chips - 1 else 0

    def to_sib(d, zs, k):
        done = meta_send.at[2, zs] if k is meta else sib_send.at[zs]
        return remote(here(d, zs, k), there(zs, c, k), done, sib_recv.at[zs, sib_slot(d, k)], i, sib)

    def lane_wait(zs, k):
        remote(there(zs, c, k), there(zs, c, k), sib_send.at[zs], lane_recv.at[zs, k], i, sib).wait_recv()

    def sib_wait(zs, k):
        mine = there(zs, 1 - c, k)
        remote(mine, mine, sib_send.at[zs], sib_recv.at[zs, k], i, sib).wait_recv()

    def sib_wait_whole(zs):
        mine = a_buf.at[CORES * zs + 1 - c]
        remote(mine, mine, sib_send.at[zs], sib_recv.at[zs, 0], i, sib).wait_recv()

    def sent_whole(sem):
        whole = a_buf.at[0]
        remote(whole, whole, sem, sib_recv.at[0, 0], i, sib).wait_send()

    def b_part(p, k):
        if k == 2:
            return meta_v.at[tiles + p]
        return b_buf.at[p, pl.ds(k * half, half)]

    def row_copy(n, k):
        source = b_part(i, k) if k == 2 else x_ref.at[pl.ds(k * half, half), 0]
        return remote(source, b_part(i, k), row_send.at[n, k], row_recv.at[i, k], (xn, yn)[n], j)

    def row_wait(p, k):
        remote(b_part(p, k), b_part(p, k), row_fwd.at[0], row_recv.at[p, k], xn, j).wait_recv()

    def row_forward(n, k):
        p, to = ((xn, yn), (yn, xn))[n]
        return remote(b_part(p, k), b_part(p, k), row_fwd.at[k], row_recv.at[p, k], to, j)

    forwards = [row_forward(0, 0), row_forward(1, 1), row_forward(0, 2)]

    def own_out(k):
        pl.when(inner_right)(lambda: to_right(0, z, k).start())
        pl.when(inner_left)(lambda: to_left(0, z, k).start())

    own_out(meta)
    row_copy(0, 2).start()
    row_copy(1, 2).start()
    lax.fori_loop(0, pieces, lambda k, n: (own_out(k), n)[1], 0)
    for k in range(2):
        row_copy(0, k).start()
        row_copy(1, 1 - k).start()
    to_sib(0, z, meta).start()
    remote(x_ref.at[:, 0], a_buf.at[j], sib_send.at[z], sib_recv.at[z, 0], i, sib).start()

    def from_left(d, k):
        lane_wait(z - d, k)
        if d < chips - 1:
            pl.when(inner_right)(lambda: to_right(d, z - d, k).start())
        to_sib(d, z - d, k).start()

    def from_right(d, k):
        lane_wait(z + d, k)
        if d < chips - 1:
            pl.when(inner_left)(lambda: to_left(d, z + d, k).start())
        to_sib(d, z + d, k).start()

    def arrive(d, k):
        pl.when(z - d >= 0)(lambda: from_left(d, k))
        pl.when(z + d <= chips - 1)(lambda: from_right(d, k))

    def arrive_loop(d):
        arrive(d, meta)
        lax.fori_loop(0, pieces, lambda k, n: (arrive(d, k), n)[1], 0)

    arrive_loop(1)
    row_wait(xn, 2)
    forwards[2].start()
    row_wait(xn, 0)
    forwards[0].start()
    row_wait(yn, 1)
    forwards[1].start()
    arrive_loop(2)
    row_wait(yn, 2)
    row_wait(dg, 2)
    row_wait(xn, 1)
    row_wait(yn, 0)
    row_wait(dg, 0)
    row_wait(dg, 1)
    own.wait()
    own_b.wait()
    oc_down.wait()

    first = z // 2
    far = (chips - 1) * (1 - first)

    def near(n):
        return n + first

    def lower(start, count):
        down = pltpu.make_async_copy(meta_v.at[pl.ds(start, count)], meta_s.at[pl.ds(start, count)], meta_loc)
        down.start()
        down.wait()

    for n in range(chips - 1):
        sib_wait(near(n), meta)
    lower(CORES * first, CORES * (chips - 1))
    lower(tiles, chips)

    def operands(m, zs):
        lhs, rhs = [], []
        for h in range(CORES):
            t = CORES * zs + h
            at = h * half + meta_s[t, 0, m]
            block = b_buf[zs, at]
            landing = meta_s[tiles + zs, 0, at]
            zero = jnp.zeros_like(block)
            rhs.append(
                jnp.concatenate([jnp.where(landing == oc_s[o, m], block, zero) for o in range(2)], axis=1)
            )
            lhs.append(a_buf[t, m])
        return lhs, rhs

    def product(m, sources):
        lhs, rhs = [], []
        for zs in sources:
            more = operands(m, zs)
            lhs += more[0]
            rhs += more[1]
        return jnp.dot(
            jnp.concatenate(lhs, axis=1), jnp.concatenate(rhs, axis=0), preferred_element_type=jnp.float32
        )

    for n in range(chips - 1):
        sib_wait_whole(near(n))

    def early(k, carry):
        for r in range(PIECE):
            m = k * PIECE + r
            acc[m] = product(m, [near(n) for n in range(chips - 1)])
        return carry

    lax.fori_loop(0, pieces, early, 0)

    is_end = jnp.logical_or(z == 0, z == chips - 1)
    not_end = jnp.logical_not(is_end)

    def far_arrive(k):
        pl.when(z == chips - 1)(lambda: from_left(chips - 1, k))
        pl.when(z == 0)(lambda: from_right(chips - 1, k))

    far_arrive(meta)
    far_arrive(0)

    for d in range(chips - 1):
        go_right = jnp.logical_and(inner_right, z - d >= 0)
        go_left = jnp.logical_and(inner_left, z + d <= chips - 1)
        pl.when(go_right)(lambda d=d: to_right(d, z - d, meta).wait_send())
        pl.when(go_left)(lambda d=d: to_left(d, z + d, meta).wait_send())
        if d < chips - 2:
            pl.when(go_right)(lambda d=d: sent_whole(right_send.at[d]))
            pl.when(go_left)(lambda d=d: sent_whole(left_send.at[d]))
        sent_whole(sib_send.at[near(d)])
        to_sib(1, near(d), meta).wait_send()
    to_sib(1, far, meta).wait_send()
    for k in range(3):
        for n in range(2):
            row_copy(n, k).wait_send()
        forwards[k].wait_send()

    sib_wait(far, meta)
    lower(CORES * far, CORES)
    pl.when(not_end)(lambda: sib_wait_whole(far))

    def late(k, carry):
        pl.when(k < pieces - 1)(lambda: far_arrive(jnp.minimum(k + 1, pieces - 1)))
        pl.when(is_end)(lambda: sib_wait(far, k))
        for r in range(PIECE):
            m = k * PIECE + r
            total = acc[m] + product(m, [far])
            for o in range(2):
                o_ref[m, o] = total[:, o * 128 : (o + 1) * 128].astype(o_ref.dtype)
        return carry

    lax.fori_loop(0, pieces, late, 0)

    d = chips - 2
    pl.when(jnp.logical_and(inner_right, z - d >= 0))(lambda: sent_whole(right_send.at[d]))
    pl.when(jnp.logical_and(inner_left, z + d <= chips - 1))(lambda: sent_whole(left_send.at[d]))
    sent_whole(sib_send.at[far])


def on_four_by_eight(xblocks, xcols, outcols):
    rows, _, size, _ = xblocks.shape
    kept = outcols.shape[1]
    slots = CORES * STEPS + STEPS
    pieces = rows // PIECE
    dma = pltpu.SemaphoreType.DMA
    return pl.pallas_call(
        kernel,
        out_shape=jax.ShapeDtypeStruct((rows, kept, size, size), jnp.bfloat16),
        in_specs=[
            pl.BlockSpec(memory_space=pltpu.VMEM),
            pl.BlockSpec(memory_space=pltpu.VMEM),
            pl.BlockSpec(memory_space=pltpu.HBM),
        ],
        out_specs=pl.BlockSpec(memory_space=pltpu.VMEM),
        scratch_shapes=[
            pltpu.VMEM((CORES * STEPS, rows, size, size), jnp.bfloat16),
            pltpu.VMEM((STEPS, rows, size, size), jnp.bfloat16),
            pltpu.VMEM((rows, size, kept * size), jnp.float32),
            pltpu.VMEM((slots, 8, 128), jnp.int32),
            pltpu.SMEM((slots, 8, 128), jnp.int32),
            pltpu.SMEM((kept, rows), jnp.int32),
            dma,
            dma((3,)),
            dma((STEPS,)),
            dma((STEPS,)),
            dma((STEPS, pieces + 1)),
            dma((STEPS,)),
            dma((STEPS, pieces + 1)),
            dma((3, STEPS)),
            dma((2, 3)),
            dma((3,)),
            dma((STEPS, 3)),
        ],
        compiler_params=pltpu.CompilerParams(
            collective_id=0, has_side_effects=True, vmem_limit_bytes=32 * 1024 * 1024
        ),
    )(xcols.T, outcols.T, xblocks)


def solution(mesh):
    in_specs = (P("row", "col", None, None), P("row", "col"), P("row", "col"))
    out_specs = P("row", "col", None, None)
    fits = mesh.shape["row"] == STEPS and mesh.shape["col"] == CORES * STEPS
    body = on_four_by_eight if fits else on_any_mesh
    return jax.shard_map(body, mesh=mesh, in_specs=in_specs, out_specs=out_specs, check_vma=False)
```

```python
import functools

import jax
import jax.numpy as jnp
from jax import lax
from jax.experimental import pallas as pl
from jax.experimental.pallas import tpu as pltpu
from jax.sharding import PartitionSpec as P

STEPS = 4
CORES = 2
PIECE = 4


def piece_sizes(rows):
    return tuple(min(PIECE, rows - start) for start in range(0, rows, PIECE))
MESH = pl.DeviceIdType.MESH


def passed_along(value, axis, steps):
    count = lax.axis_size(axis)
    pairs = [(source, (source + steps) % count) for source in range(count)]
    return lax.ppermute(value, axis, pairs)


def broadcast(value, axis, source):
    kept = jnp.where(lax.axis_index(axis) == source, value, 0).astype(value.dtype)
    return lax.psum(kept, axis)


def add_products(total, a_blocks, a_cols, b_blocks, b_cols, targets, offset):
    index = offset + a_cols
    chosen = jnp.take(b_blocks, index, axis=0)
    landing = jnp.take(b_cols, index, axis=0)
    product = jnp.einsum("mab,mbc->mac", a_blocks, chosen, preferred_element_type=jnp.float32)
    weight = (landing[:, None] == targets).astype(jnp.float32)
    return total + weight[:, :, None, None] * product[:, None]


def on_any_mesh(xblocks, xcols, outcols):
    row_count = lax.axis_size("row")
    col_count = lax.axis_size("col")
    per_panel = col_count // row_count
    block_rows = xblocks.shape[0]
    tile_cols = block_rows // per_panel
    block_size = xblocks.shape[2]
    kept = outcols.shape[1]
    row_here = lax.axis_index("row")
    own_blocks = xblocks[:, 0]
    own_cols = xcols[:, 0]
    total = jnp.zeros((block_rows, kept, block_size, block_size), jnp.float32)
    moving = (own_blocks, own_cols)
    for step_no in range(STEPS):
        panel = (row_here + step_no) % row_count
        if step_no > 0:
            moving = passed_along((moving[0], moving[1]), "row", -1)
        for half_no in range(per_panel):
            tile_blocks, tile_cols_ids = (
                broadcast(own_blocks, "col", per_panel * panel + half_no),
                broadcast(own_cols, "col", per_panel * panel + half_no),
            )
            total = add_products(
                total,
                tile_blocks,
                tile_cols_ids,
                moving[0],
                moving[1],
                outcols,
                half_no * tile_cols,
            )
    return total.astype(jnp.bfloat16)


def remote(src, dst, send_sem, recv_sem, row, col):
    return pltpu.make_async_remote_copy(
        src_ref=src,
        dst_ref=dst,
        send_sem=send_sem,
        recv_sem=recv_sem,
        device_id=(row, col),
        device_id_type=MESH,
    )


def kernel(
    xc_ref, oc_ref, x_ref, o_ref,
    a_buf, b_buf, acc, meta_v, meta_s, oc_s,
    meta_loc, own_loc,
    right_send, left_send, lane_recv, sib_send, sib_recv, meta_send,
    row_send, row_fwd, row_recv,
):
    rows = x_ref.shape[0]
    half = rows // 2
    chips = STEPS
    sizes = piece_sizes(rows)
    pieces = len(sizes)
    meta = pieces
    i = lax.axis_index("row")
    j = lax.axis_index("col")
    z, c = j // CORES, j % CORES
    y, x = i // 2, i % 2
    xn = 2 * y + (1 - x)
    yn = 2 * (1 - y) + x
    dg = 2 * (1 - y) + (1 - x)
    sib = j + 1 - 2 * c
    right, left = j + CORES, j - CORES
    inner_right = z < chips - 1
    inner_left = z > 0
    tiles = CORES * chips

    barrier = pltpu.get_barrier_semaphore()

    def greet(row, col):
        pl.semaphore_signal(barrier, inc=1, device_id=(row, col), device_id_type=MESH)

    greet(i, sib)
    pl.when(inner_right)(lambda: greet(i, right))
    pl.when(inner_left)(lambda: greet(i, left))
    greet(xn, j)
    greet(yn, j)

    own = pltpu.make_async_copy(x_ref.at[:, 0], a_buf.at[j], own_loc.at[0])
    own_b = pltpu.make_async_copy(x_ref.at[:, 0], b_buf.at[i], own_loc.at[1])
    own.start()
    own_b.start()
    oc_down = pltpu.make_async_copy(oc_ref, oc_s, own_loc.at[2])
    oc_down.start()
    meta_v[j, 0:1, 0:rows] = xc_ref[...]
    meta_v[tiles + i, 0:1, 0:rows] = xc_ref[...]
    pl.semaphore_wait(barrier, 5 - jnp.where(jnp.logical_and(inner_left, inner_right), 0, 1))

    def part(k):
        return pl.ds(sum(sizes[:k]), sizes[k])

    def there(zs, core, k):
        if k == meta:
            return meta_v.at[CORES * zs + core]
        return a_buf.at[CORES * zs + core, part(k)]

    def here(d, zs, k):
        if k == meta or d != 0:
            return there(zs, c, k)
        return x_ref.at[part(k), 0]

    def to_right(d, zs, k):
        done = meta_send.at[0, d] if k == meta else right_send.at[d]
        return remote(here(d, zs, k), there(zs, c, k), done, lane_recv.at[zs, k], i, right)

    def to_left(d, zs, k):
        done = meta_send.at[1, d] if k == meta else left_send.at[d]
        return remote(here(d, zs, k), there(zs, c, k), done, lane_recv.at[zs, k], i, left)

    def sib_slot(d, k):
        return k if k == meta or d == chips - 1 else 0

    def to_sib(d, zs, k):
        done = meta_send.at[2, zs] if k == meta else sib_send.at[zs]
        return remote(here(d, zs, k), there(zs, c, k), done, sib_recv.at[zs, sib_slot(d, k)], i, sib)

    def lane_wait(zs, k):
        remote(there(zs, c, k), there(zs, c, k), sib_send.at[zs], lane_recv.at[zs, k], i, sib).wait_recv()

    def sib_wait(zs, k):
        mine = there(zs, 1 - c, k)
        remote(mine, mine, sib_send.at[zs], sib_recv.at[zs, k], i, sib).wait_recv()

    def sib_wait_whole(zs):
        mine = a_buf.at[CORES * zs + 1 - c]
        remote(mine, mine, sib_send.at[zs], sib_recv.at[zs, 0], i, sib).wait_recv()

    def sent_whole(sem):
        whole = a_buf.at[0]
        remote(whole, whole, sem, sib_recv.at[0, 0], i, sib).wait_send()

    def b_part(p, k):
        if k == 2:
            return meta_v.at[tiles + p]
        return b_buf.at[p, pl.ds(k * half, half)]

    def row_copy(n, k):
        source = b_part(i, k) if k == 2 else x_ref.at[pl.ds(k * half, half), 0]
        return remote(source, b_part(i, k), row_send.at[n, k], row_recv.at[i, k], (xn, yn)[n], j)

    def row_wait(p, k):
        remote(b_part(p, k), b_part(p, k), row_fwd.at[0], row_recv.at[p, k], xn, j).wait_recv()

    def row_forward(n, k):
        p, to = ((xn, yn), (yn, xn))[n]
        return remote(b_part(p, k), b_part(p, k), row_fwd.at[k], row_recv.at[p, k], to, j)

    forwards = [row_forward(0, 0), row_forward(1, 1), row_forward(0, 2)]

    def own_out(k):
        pl.when(inner_right)(lambda: to_right(0, z, k).start())
        pl.when(inner_left)(lambda: to_left(0, z, k).start())

    own_out(meta)
    row_copy(0, 2).start()
    row_copy(1, 2).start()
    for k in range(pieces):
        own_out(k)
    for k in range(2):
        row_copy(0, k).start()
        row_copy(1, 1 - k).start()
    to_sib(0, z, meta).start()
    remote(x_ref.at[:, 0], a_buf.at[j], sib_send.at[z], sib_recv.at[z, 0], i, sib).start()

    def from_left(d, k):
        lane_wait(z - d, k)
        if d < chips - 1:
            pl.when(inner_right)(lambda: to_right(d, z - d, k).start())
        to_sib(d, z - d, k).start()

    def from_right(d, k):
        lane_wait(z + d, k)
        if d < chips - 1:
            pl.when(inner_left)(lambda: to_left(d, z + d, k).start())
        to_sib(d, z + d, k).start()

    def arrive(d, k):
        pl.when(z - d >= 0)(lambda: from_left(d, k))
        pl.when(z + d <= chips - 1)(lambda: from_right(d, k))

    def arrive_loop(d):
        arrive(d, meta)
        for k in range(pieces):
            arrive(d, k)

    arrive_loop(1)
    row_wait(xn, 2)
    forwards[2].start()
    row_wait(xn, 0)
    forwards[0].start()
    row_wait(yn, 1)
    forwards[1].start()
    arrive_loop(2)
    row_wait(yn, 2)
    row_wait(dg, 2)
    row_wait(xn, 1)
    row_wait(yn, 0)
    row_wait(dg, 0)
    row_wait(dg, 1)
    own.wait()
    own_b.wait()
    oc_down.wait()

    first = z // 2
    far = (chips - 1) * (1 - first)

    def near(n):
        return n + first

    def lower(start, count):
        down = pltpu.make_async_copy(meta_v.at[pl.ds(start, count)], meta_s.at[pl.ds(start, count)], meta_loc)
        down.start()
        down.wait()

    for n in range(chips - 1):
        sib_wait(near(n), meta)
    lower(CORES * first, CORES * (chips - 1))
    lower(tiles, chips)

    def operands(m, zs):
        lhs, rhs = [], []
        for h in range(CORES):
            t = CORES * zs + h
            at = h * half + meta_s[t, 0, m]
            block = b_buf[zs, at]
            landing = meta_s[tiles + zs, 0, at]
            zero = jnp.zeros_like(block)
            rhs.append(
                jnp.concatenate([jnp.where(landing == oc_s[o, m], block, zero) for o in range(2)], axis=1)
            )
            lhs.append(a_buf[t, m])
        return lhs, rhs

    def product(m, sources):
        lhs, rhs = [], []
        for zs in sources:
            more = operands(m, zs)
            lhs += more[0]
            rhs += more[1]
        return jnp.dot(
            jnp.concatenate(lhs, axis=1), jnp.concatenate(rhs, axis=0), preferred_element_type=jnp.float32
        )

    for n in range(chips - 1):
        sib_wait_whole(near(n))

    def early(m, carry):
        acc[m] = product(m, [near(n) for n in range(chips - 1)])
        return carry

    lax.fori_loop(0, rows, early, 0)

    is_end = jnp.logical_or(z == 0, z == chips - 1)
    not_end = jnp.logical_not(is_end)

    def far_arrive(k):
        pl.when(z == chips - 1)(lambda: from_left(chips - 1, k))
        pl.when(z == 0)(lambda: from_right(chips - 1, k))

    far_arrive(meta)
    far_arrive(0)

    for d in range(chips - 1):
        go_right = jnp.logical_and(inner_right, z - d >= 0)
        go_left = jnp.logical_and(inner_left, z + d <= chips - 1)
        pl.when(go_right)(lambda d=d: to_right(d, z - d, meta).wait_send())
        pl.when(go_left)(lambda d=d: to_left(d, z + d, meta).wait_send())
        if d < chips - 2:
            pl.when(go_right)(lambda d=d: sent_whole(right_send.at[d]))
            pl.when(go_left)(lambda d=d: sent_whole(left_send.at[d]))
        sent_whole(sib_send.at[near(d)])
        to_sib(1, near(d), meta).wait_send()
    to_sib(1, far, meta).wait_send()
    for k in range(3):
        for n in range(2):
            row_copy(n, k).wait_send()
        forwards[k].wait_send()

    sib_wait(far, meta)
    lower(CORES * far, CORES)
    pl.when(not_end)(lambda: sib_wait_whole(far))

    def late(m, carry):
        total = acc[m] + product(m, [far])
        for o in range(2):
            o_ref[m, o] = total[:, o * 128 : (o + 1) * 128].astype(o_ref.dtype)
        return carry

    for k in range(pieces):
        if k < pieces - 1:
            far_arrive(k + 1)
        pl.when(is_end)(lambda k=k: sib_wait(far, k))
        start = sum(sizes[:k])
        lax.fori_loop(start, start + sizes[k], late, 0, unroll=True)

    d = chips - 2
    pl.when(jnp.logical_and(inner_right, z - d >= 0))(lambda: sent_whole(right_send.at[d]))
    pl.when(jnp.logical_and(inner_left, z + d <= chips - 1))(lambda: sent_whole(left_send.at[d]))
    sent_whole(sib_send.at[far])


def on_four_by_eight(xblocks, xcols, outcols):
    rows, _, size, _ = xblocks.shape
    kept = outcols.shape[1]
    slots = CORES * STEPS + STEPS
    pieces = len(piece_sizes(rows))
    dma = pltpu.SemaphoreType.DMA
    return pl.pallas_call(
        kernel,
        out_shape=jax.ShapeDtypeStruct((rows, kept, size, size), jnp.bfloat16),
        in_specs=[
            pl.BlockSpec(memory_space=pltpu.VMEM),
            pl.BlockSpec(memory_space=pltpu.VMEM),
            pl.BlockSpec(memory_space=pltpu.HBM),
        ],
        out_specs=pl.BlockSpec(memory_space=pltpu.VMEM),
        scratch_shapes=[
            pltpu.VMEM((CORES * STEPS, rows, size, size), jnp.bfloat16),
            pltpu.VMEM((STEPS, rows, size, size), jnp.bfloat16),
            pltpu.VMEM((rows, size, kept * size), jnp.float32),
            pltpu.VMEM((slots, 8, 128), jnp.int32),
            pltpu.SMEM((slots, 8, 128), jnp.int32),
            pltpu.SMEM((kept, rows), jnp.int32),
            dma,
            dma((3,)),
            dma((STEPS,)),
            dma((STEPS,)),
            dma((STEPS, pieces + 1)),
            dma((STEPS,)),
            dma((STEPS, pieces + 1)),
            dma((3, STEPS)),
            dma((2, 3)),
            dma((3,)),
            dma((STEPS, 3)),
        ],
        compiler_params=pltpu.CompilerParams(
            collective_id=0, has_side_effects=True, vmem_limit_bytes=32 * 1024 * 1024
        ),
    )(xcols.T, outcols.T, xblocks)


def solution(mesh):
    in_specs = (P("row", "col", None, None), P("row", "col"), P("row", "col"))
    out_specs = P("row", "col", None, None)
    fits = mesh.shape["row"] == STEPS and mesh.shape["col"] == CORES * STEPS
    body = on_four_by_eight if fits else on_any_mesh
    return jax.shard_map(body, mesh=mesh, in_specs=in_specs, out_specs=out_specs, check_vma=False)
```

```python
import functools

import jax
import jax.numpy as jnp
from jax import lax
from jax.experimental import pallas as pl
from jax.experimental.pallas import tpu as pltpu
from jax.sharding import PartitionSpec as P

STEPS = 4
CORES = 2
PIECE = 4


def piece_sizes(rows):
    return tuple(min(PIECE, rows - start) for start in range(0, rows, PIECE))
MESH = pl.DeviceIdType.MESH


def passed_along(value, axis, steps):
    count = lax.axis_size(axis)
    pairs = [(source, (source + steps) % count) for source in range(count)]
    return lax.ppermute(value, axis, pairs)


def broadcast(value, axis, source):
    kept = jnp.where(lax.axis_index(axis) == source, value, 0).astype(value.dtype)
    return lax.psum(kept, axis)


def add_products(total, a_blocks, a_cols, b_blocks, b_cols, targets, offset):
    index = offset + a_cols
    chosen = jnp.take(b_blocks, index, axis=0)
    landing = jnp.take(b_cols, index, axis=0)
    product = jnp.einsum("mab,mbc->mac", a_blocks, chosen, preferred_element_type=jnp.float32)
    weight = (landing[:, None] == targets).astype(jnp.float32)
    return total + weight[:, :, None, None] * product[:, None]


def on_any_mesh(xblocks, xcols, outcols):
    row_count = lax.axis_size("row")
    col_count = lax.axis_size("col")
    per_panel = col_count // row_count
    block_rows = xblocks.shape[0]
    tile_cols = block_rows // per_panel
    block_size = xblocks.shape[2]
    kept = outcols.shape[1]
    row_here = lax.axis_index("row")
    own_blocks = xblocks[:, 0]
    own_cols = xcols[:, 0]
    total = jnp.zeros((block_rows, kept, block_size, block_size), jnp.float32)
    moving = (own_blocks, own_cols)
    for step_no in range(STEPS):
        panel = (row_here + step_no) % row_count
        if step_no > 0:
            moving = passed_along((moving[0], moving[1]), "row", -1)
        for half_no in range(per_panel):
            tile_blocks, tile_cols_ids = (
                broadcast(own_blocks, "col", per_panel * panel + half_no),
                broadcast(own_cols, "col", per_panel * panel + half_no),
            )
            total = add_products(
                total,
                tile_blocks,
                tile_cols_ids,
                moving[0],
                moving[1],
                outcols,
                half_no * tile_cols,
            )
    return total.astype(jnp.bfloat16)


def remote(src, dst, send_sem, recv_sem, row, col):
    return pltpu.make_async_remote_copy(
        src_ref=src,
        dst_ref=dst,
        send_sem=send_sem,
        recv_sem=recv_sem,
        device_id=(row, col),
        device_id_type=MESH,
    )


def kernel(
    xc_ref, oc_ref, x_ref, o_ref,
    a_buf, b_buf, acc, meta_v, meta_s, oc_s,
    meta_loc, own_loc,
    right_send, left_send, lane_recv, sib_send, sib_recv, meta_send,
    row_send, row_fwd, row_recv,
):
    rows = x_ref.shape[0]
    half = rows // 2
    chips = STEPS
    sizes = piece_sizes(rows)
    pieces = len(sizes)
    meta = pieces
    i = lax.axis_index("row")
    j = lax.axis_index("col")
    z, c = j // CORES, j % CORES
    y, x = i // 2, i % 2
    xn = 2 * y + (1 - x)
    yn = 2 * (1 - y) + x
    dg = 2 * (1 - y) + (1 - x)
    sib = j + 1 - 2 * c
    right, left = j + CORES, j - CORES
    inner_right = z < chips - 1
    inner_left = z > 0
    tiles = CORES * chips

    barrier = pltpu.get_barrier_semaphore()

    def greet(row, col):
        pl.semaphore_signal(barrier, inc=1, device_id=(row, col), device_id_type=MESH)

    pl.when(inner_right)(lambda: greet(i, right))
    pl.when(inner_left)(lambda: greet(i, left))
    greet(i, sib)
    greet(xn, j)
    greet(yn, j)

    own = pltpu.make_async_copy(x_ref.at[:, 0], a_buf.at[j], own_loc.at[0])
    own_b = pltpu.make_async_copy(x_ref.at[:, 0], b_buf.at[i], own_loc.at[1])
    own.start()
    own_b.start()
    oc_down = pltpu.make_async_copy(oc_ref, oc_s, own_loc.at[2])
    oc_down.start()
    meta_v[j, 0:1, 0:rows] = xc_ref[...]
    meta_v[tiles + i, 0:1, 0:rows] = xc_ref[...]
    pl.semaphore_wait(barrier, 5 - jnp.where(jnp.logical_and(inner_left, inner_right), 0, 1))

    def part(k):
        return pl.ds(sum(sizes[:k]), sizes[k])

    def there(zs, core, k):
        if k == meta:
            return meta_v.at[CORES * zs + core]
        return a_buf.at[CORES * zs + core, part(k)]

    def here(d, zs, k):
        if k == meta or d != 0:
            return there(zs, c, k)
        return x_ref.at[part(k), 0]

    def to_right(d, zs, k):
        done = meta_send.at[0, d] if k == meta else right_send.at[d]
        return remote(here(d, zs, k), there(zs, c, k), done, lane_recv.at[zs, k], i, right)

    def to_left(d, zs, k):
        done = meta_send.at[1, d] if k == meta else left_send.at[d]
        return remote(here(d, zs, k), there(zs, c, k), done, lane_recv.at[zs, k], i, left)

    def sib_slot(d, k):
        return k if k == meta or d == chips - 1 else 0

    def to_sib(d, zs, k):
        done = meta_send.at[2, zs] if k == meta else sib_send.at[zs]
        return remote(here(d, zs, k), there(zs, c, k), done, sib_recv.at[zs, sib_slot(d, k)], i, sib)

    def lane_wait(zs, k):
        remote(there(zs, c, k), there(zs, c, k), sib_send.at[zs], lane_recv.at[zs, k], i, sib).wait_recv()

    def sib_wait(zs, k):
        mine = there(zs, 1 - c, k)
        remote(mine, mine, sib_send.at[zs], sib_recv.at[zs, k], i, sib).wait_recv()

    def sib_wait_whole(zs):
        mine = a_buf.at[CORES * zs + 1 - c]
        remote(mine, mine, sib_send.at[zs], sib_recv.at[zs, 0], i, sib).wait_recv()

    def sent_whole(sem):
        whole = a_buf.at[0]
        remote(whole, whole, sem, sib_recv.at[0, 0], i, sib).wait_send()

    def b_part(p, k):
        if k == 2:
            return meta_v.at[tiles + p]
        return b_buf.at[p, pl.ds(k * half, half)]

    def row_copy(n, k):
        source = b_part(i, k) if k == 2 else x_ref.at[pl.ds(k * half, half), 0]
        return remote(source, b_part(i, k), row_send.at[n, k], row_recv.at[i, k], (xn, yn)[n], j)

    def row_wait(p, k):
        remote(b_part(p, k), b_part(p, k), row_fwd.at[0], row_recv.at[p, k], xn, j).wait_recv()

    def row_forward(n, k):
        p, to = ((xn, yn), (yn, xn))[n]
        return remote(b_part(p, k), b_part(p, k), row_fwd.at[k], row_recv.at[p, k], to, j)

    forwards = [row_forward(0, 0), row_forward(1, 1), row_forward(0, 2)]

    def own_out(k):
        pl.when(inner_right)(lambda: to_right(0, z, k).start())
        pl.when(inner_left)(lambda: to_left(0, z, k).start())

    own_out(0)
    own_out(meta)
    for k in range(1, pieces):
        own_out(k)
    row_copy(0, 2).start()
    row_copy(1, 2).start()
    for k in range(2):
        row_copy(0, k).start()
        row_copy(1, 1 - k).start()
    to_sib(0, z, meta).start()
    remote(x_ref.at[:, 0], a_buf.at[j], sib_send.at[z], sib_recv.at[z, 0], i, sib).start()

    def from_left(d, k):
        lane_wait(z - d, k)
        if d < chips - 1:
            pl.when(inner_right)(lambda: to_right(d, z - d, k).start())
        to_sib(d, z - d, k).start()

    def from_right(d, k):
        lane_wait(z + d, k)
        if d < chips - 1:
            pl.when(inner_left)(lambda: to_left(d, z + d, k).start())
        to_sib(d, z + d, k).start()

    def arrive(d, k):
        pl.when(z - d >= 0)(lambda: from_left(d, k))
        pl.when(z + d <= chips - 1)(lambda: from_right(d, k))

    def arrive_loop(d):
        arrive(d, 0)
        arrive(d, meta)
        for k in range(1, pieces):
            arrive(d, k)

    arrive_loop(1)
    row_wait(xn, 2)
    forwards[2].start()
    row_wait(xn, 0)
    forwards[0].start()
    row_wait(yn, 1)
    forwards[1].start()
    arrive_loop(2)
    row_wait(yn, 2)
    row_wait(dg, 2)
    row_wait(xn, 1)
    row_wait(yn, 0)
    row_wait(dg, 0)
    row_wait(dg, 1)
    own.wait()
    own_b.wait()
    oc_down.wait()

    first = z // 2
    far = (chips - 1) * (1 - first)

    def near(n):
        return n + first

    def lower(start, count):
        down = pltpu.make_async_copy(meta_v.at[pl.ds(start, count)], meta_s.at[pl.ds(start, count)], meta_loc)
        down.start()
        down.wait()

    for n in range(chips - 1):
        sib_wait(near(n), meta)
    lower(CORES * first, CORES * (chips - 1))
    lower(tiles, chips)

    def operands(m, zs):
        lhs, rhs = [], []
        for h in range(CORES):
            t = CORES * zs + h
            at = h * half + meta_s[t, 0, m]
            block = b_buf[zs, at]
            landing = meta_s[tiles + zs, 0, at]
            zero = jnp.zeros_like(block)
            rhs.append(
                jnp.concatenate([jnp.where(landing == oc_s[o, m], block, zero) for o in range(2)], axis=1)
            )
            lhs.append(a_buf[t, m])
        return lhs, rhs

    def product(m, sources):
        lhs, rhs = [], []
        for zs in sources:
            more = operands(m, zs)
            lhs += more[0]
            rhs += more[1]
        return jnp.dot(
            jnp.concatenate(lhs, axis=1), jnp.concatenate(rhs, axis=0), preferred_element_type=jnp.float32
        )

    for n in range(chips - 1):
        sib_wait_whole(near(n))

    def early(m, carry):
        acc[m] = product(m, [near(n) for n in range(chips - 1)])
        return carry

    lax.fori_loop(0, rows, early, 0)

    is_end = jnp.logical_or(z == 0, z == chips - 1)
    not_end = jnp.logical_not(is_end)

    def far_arrive(k):
        pl.when(z == chips - 1)(lambda: from_left(chips - 1, k))
        pl.when(z == 0)(lambda: from_right(chips - 1, k))

    far_arrive(0)
    far_arrive(meta)

    for d in range(chips - 1):
        go_right = jnp.logical_and(inner_right, z - d >= 0)
        go_left = jnp.logical_and(inner_left, z + d <= chips - 1)
        pl.when(go_right)(lambda d=d: to_right(d, z - d, meta).wait_send())
        pl.when(go_left)(lambda d=d: to_left(d, z + d, meta).wait_send())
        if d < chips - 2:
            pl.when(go_right)(lambda d=d: sent_whole(right_send.at[d]))
            pl.when(go_left)(lambda d=d: sent_whole(left_send.at[d]))
        sent_whole(sib_send.at[near(d)])
        to_sib(1, near(d), meta).wait_send()
    to_sib(1, far, meta).wait_send()
    for k in range(3):
        for n in range(2):
            row_copy(n, k).wait_send()
        forwards[k].wait_send()

    sib_wait(far, meta)
    lower(CORES * far, CORES)
    pl.when(not_end)(lambda: sib_wait_whole(far))

    def late(m, carry):
        total = acc[m] + product(m, [far])
        for o in range(2):
            o_ref[m, o] = total[:, o * 128 : (o + 1) * 128].astype(o_ref.dtype)
        return carry

    for k in range(pieces):
        if k < pieces - 1:
            far_arrive(k + 1)
        pl.when(is_end)(lambda k=k: sib_wait(far, k))
        start = sum(sizes[:k])
        lax.fori_loop(start, start + sizes[k], late, 0, unroll=True)

    d = chips - 2
    pl.when(jnp.logical_and(inner_right, z - d >= 0))(lambda: sent_whole(right_send.at[d]))
    pl.when(jnp.logical_and(inner_left, z + d <= chips - 1))(lambda: sent_whole(left_send.at[d]))
    sent_whole(sib_send.at[far])


def on_four_by_eight(xblocks, xcols, outcols):
    rows, _, size, _ = xblocks.shape
    kept = outcols.shape[1]
    slots = CORES * STEPS + STEPS
    pieces = len(piece_sizes(rows))
    dma = pltpu.SemaphoreType.DMA
    return pl.pallas_call(
        kernel,
        out_shape=jax.ShapeDtypeStruct((rows, kept, size, size), jnp.bfloat16),
        in_specs=[
            pl.BlockSpec(memory_space=pltpu.VMEM),
            pl.BlockSpec(memory_space=pltpu.VMEM),
            pl.BlockSpec(memory_space=pltpu.HBM),
        ],
        out_specs=pl.BlockSpec(memory_space=pltpu.VMEM),
        scratch_shapes=[
            pltpu.VMEM((CORES * STEPS, rows, size, size), jnp.bfloat16),
            pltpu.VMEM((STEPS, rows, size, size), jnp.bfloat16),
            pltpu.VMEM((rows, size, kept * size), jnp.float32),
            pltpu.VMEM((slots, 8, 128), jnp.int32),
            pltpu.SMEM((slots, 8, 128), jnp.int32),
            pltpu.SMEM((kept, rows), jnp.int32),
            dma,
            dma((3,)),
            dma((STEPS,)),
            dma((STEPS,)),
            dma((STEPS, pieces + 1)),
            dma((STEPS,)),
            dma((STEPS, pieces + 1)),
            dma((3, STEPS)),
            dma((2, 3)),
            dma((3,)),
            dma((STEPS, 3)),
        ],
        compiler_params=pltpu.CompilerParams(
            collective_id=0, has_side_effects=True, vmem_limit_bytes=32 * 1024 * 1024
        ),
    )(xcols.T, outcols.T, xblocks)


def solution(mesh):
    in_specs = (P("row", "col", None, None), P("row", "col"), P("row", "col"))
    out_specs = P("row", "col", None, None)
    fits = mesh.shape["row"] == STEPS and mesh.shape["col"] == CORES * STEPS
    body = on_four_by_eight if fits else on_any_mesh
    return jax.shard_map(body, mesh=mesh, in_specs=in_specs, out_specs=out_specs, check_vma=False)
```
